32 devices in a mesh: groups: 2 (over y), rows: 4 (over z), cols: 2 (over x), sub: 2 (over core).
Axes of the slice: x: 2, y: 2, z: 4, core: 2. Of those that a mesh axis runs over, the one named last changes fastest.
Arguments:
- features: bfloat16 [128, 256, 512], P(None, ('groups', 'rows'), ('cols', 'sub')), parts along dimension 1, may hold values from -9 to 9
- guide_image: bfloat16 [3, 256, 512], P(None, ('groups', 'rows'), ('cols', 'sub')), parts along dimension 1, may hold values from 0 to 1
- conv_weight: bfloat16 [3, 3, 64, 128], replicated, may hold values from -0.1875 to 0.1875
- head_weight: float32 [2, 64], replicated, may hold values from -0.75 to 0.75
- pixel_mask: int32 [256, 512], P(('groups', 'rows', 'cols', 'sub')), parts along dimension 0, may hold values 0 or 1
Outputs:
- mixture: float32 [256, 512], P(('groups', 'rows', 'cols', 'sub')), parts along dimension 0
The draws below stay inside these ranges and needn't reach their ends.
There are 2 independent parts, one for each index of `groups`. The reference program is written for one: setup_inputs(seed, part) draws one part's arguments, and reference() takes and returns one part's arrays. A program takes and returns all parts, laid end to end along the dimension named above; an argument that names none is the same for every part. Nothing has to cross between parts.
All inputs are finite; a program needn't handle non-finite values. No bound on the sum of `pixel_mask` on one device may be relied on, other than what follows from the above.
Results may differ from the reference program's by a relative error of at most 0.0003.
Values may be sent and summed in bfloat16 or wider, within the bound.
A program may use at most 64 MiB of HBM per device.

```python
import jax
import jax.numpy as jnp
from jax import lax

C_IN = 128
C_MID = 64
ITERS = 2
PICTURE_HEIGHT = 128
NW = 512


def draw_features(key, part):
    random_pick = jnp.clip(jax.random.normal(key, (C_IN, PICTURE_HEIGHT, NW), jnp.float32), -6.0, 6.0)
    row_index = jnp.arange(PICTURE_HEIGHT, dtype=jnp.float32)
    row_scale = 0.5 * (1.0 + 2.0 * row_index / max(PICTURE_HEIGHT - 1, 1))
    return (random_pick * row_scale[None, :, None]).astype(jnp.bfloat16)


def set_ends(entries, own_key, least, high):
    place = [jax.random.randint(jax.random.fold_in(own_key, axis), (), 0, length) for axis, length in enumerate(entries.shape)]
    main_axis = entries.shape.index(max(entries.shape))
    beside = place[:main_axis] + [(place[main_axis] + 1) % entries.shape[main_axis]] + place[main_axis + 1:]
    return entries.at[tuple(place)].set(least).at[tuple(beside)].set(high)


def shard_levels(key, dims, cuts, low, largest):
    def one(axis_at, shards_of):
        heights = jax.random.uniform(jax.random.fold_in(jax.random.fold_in(key, 6), axis_at), (shards_of,), jnp.float32, low / len(cuts), largest / len(cuts))
        return jnp.repeat(jnp.exp(heights), dims[axis_at] // shards_of).reshape((-1,) + (1,) * (len(dims) - axis_at - 1))

    gain = one(*cuts[0])
    for cut in cuts[1:]:
        gain = gain * one(*cut)
    return gain


def gaussian(own_key, dims, spread, limit, kind=jnp.bfloat16):
    array = spread * jax.random.normal(own_key, dims, jnp.float32)
    return jnp.clip(array, min=-limit, max=limit).astype(kind)


def setup_inputs(seed: int = 0, part: int = 0) -> dict:
    key_of = jax.random.split(jax.random.key(seed), 6)
    part_splits = jax.random.split(jax.random.fold_in(key_of[5], part), 6)
    features = draw_features(jax.random.fold_in(jax.random.fold_in(key_of[5], part), 71), part)
    guide_image = jnp.clip(1.0 * jax.random.uniform(part_splits[1], (3, PICTURE_HEIGHT, NW), jnp.float32) ** shard_levels(part_splits[1], (3, PICTURE_HEIGHT, NW), ((1, 4), (2, 4)), -0.2, 0.2), 0.0, 1.0).astype(jnp.bfloat16)
    conv_weight = gaussian(key_of[2], (3, 3, C_MID, C_IN), (9 * C_IN) ** -0.5, 0.1875)
    head_weight = gaussian(key_of[3], (2, C_MID), C_MID ** -0.5, 0.75, jnp.float32)
    pixel_mask = set_ends((jax.random.randint(part_splits[4], (PICTURE_HEIGHT, NW), 0, 2) < 1).astype(jnp.int32), jax.random.fold_in(part_splits[4], 1), 0, 1)
    return dict(features=features, guide_image=guide_image, conv_weight=conv_weight, head_weight=head_weight, pixel_mask=pixel_mask)


RIDGE = 0.05
BASE_WEIGHT = 0.1


def box_sum(extended):
    vertical = extended[:, :-2, :] + extended[:, 1:-1, :] + extended[:, 2:, :]
    return vertical[:, :, :-2] + vertical[:, :, 1:-1] + vertical[:, :, 2:]


def window_stats(guide_ext):
    average = box_sum(guide_ext) / 9.0
    red_ext, green_ext, blue_ext = guide_ext[0], guide_ext[1], guide_ext[2]
    products = jnp.stack([red_ext * red_ext, red_ext * green_ext, red_ext * blue_ext, green_ext * green_ext, green_ext * blue_ext, blue_ext * blue_ext])
    second = box_sum(products) / 9.0
    cov_rr = second[0] - average[0] * average[0] + RIDGE
    cov_rg = second[1] - average[0] * average[1]
    joint_spread_redyellow = second[2] - average[0] * average[2]
    cov_gg = second[3] - average[1] * average[1] + RIDGE
    covariance_green_blue = second[4] - average[1] * average[2]
    cov_bb = second[5] - average[2] * average[2] + RIDGE
    cof_rr = cov_gg * cov_bb - covariance_green_blue * covariance_green_blue
    cof_rg = joint_spread_redyellow * covariance_green_blue - cov_rg * cov_bb
    cof_rb = cov_rg * covariance_green_blue - joint_spread_redyellow * cov_gg
    cof_gg = cov_rr * cov_bb - joint_spread_redyellow * joint_spread_redyellow
    cofactor_green_blue = cov_rg * joint_spread_redyellow - cov_rr * covariance_green_blue
    cof_bb = cov_rr * cov_gg - cov_rg * cov_rg
    determinant = cov_rr * cof_rr + cov_rg * cof_rg + joint_spread_redyellow * cof_rb
    inverse = jnp.stack([cof_rr, cof_rg, cof_rb, cof_gg, cofactor_green_blue, cof_bb]) / determinant
    return average, inverse


def coefficients(field_ext, guide_ext, average, inverse):
    field_box = box_sum(field_ext)[0] / 9.0
    crossed = box_sum(guide_ext * field_ext) / 9.0 - average * field_box
    slope_r = inverse[0] * crossed[0] + inverse[1] * crossed[1] + inverse[2] * crossed[2]
    slope_g = inverse[1] * crossed[0] + inverse[3] * crossed[1] + inverse[4] * crossed[2]
    gradient_coefficient_third = inverse[2] * crossed[0] + inverse[4] * crossed[1] + inverse[5] * crossed[2]
    offset = field_box - (slope_r * average[0] + slope_g * average[1] + gradient_coefficient_third * average[2])
    return jnp.stack([slope_r, slope_g, gradient_coefficient_third, offset])


def apply_operator(field_map, coef_ext, guide_local_tile, weights):
    summed = box_sum(coef_ext)
    smooth = summed[0] * guide_local_tile[0] + summed[1] * guide_local_tile[1] + summed[2] * guide_local_tile[2] + summed[3]
    return 9.0 * field_map - smooth + weights * field_map


def head_maps(extended, conv_weight, head_weight, height, columns):
    channels = extended.shape[0]
    accumulated = jnp.zeros((conv_weight.shape[2], height * columns), jnp.float32)
    for shift_r in range(3):
        for shift_c in range(3):
            window_cell_count = extended[:, shift_r:shift_r + height, shift_c:shift_c + columns].reshape(channels, height * columns)
            accumulated = accumulated + jnp.dot(conv_weight[shift_r, shift_c], window_cell_count, preferred_element_type=jnp.float32)
    hidden = jnp.maximum(accumulated, 0.0)
    logits = jnp.dot(head_weight, hidden, precision=lax.Precision.HIGHEST)
    seed_map = jax.nn.sigmoid(logits[0])
    certainty = jax.nn.softplus(logits[1])
    return jnp.stack([seed_map, certainty]).reshape(2, height, columns)


def pad_all(stack):
    return jnp.pad(stack, ((0, 0), (1, 1), (1, 1)))


def reference(features, guide_image, conv_weight, head_weight, pixel_mask):
    padded = pad_all(features)
    block_rows = 16
    block_count = PICTURE_HEIGHT // block_rows

    def one_block(block_index):
        first_row = (block_index * block_rows).astype(jnp.int32)
        rows_in = lax.dynamic_slice_in_dim(padded, first_row, block_rows + 2, 1)
        return head_maps(rows_in, conv_weight, head_weight, block_rows, NW)

    predictor_result = lax.map(one_block, jnp.arange(block_count, dtype=jnp.int32))
    predictor_result = jnp.transpose(predictor_result, (1, 0, 2, 3)).reshape(2, PICTURE_HEIGHT, NW)
    seed_map, certainty = predictor_result[0], predictor_result[1]
    guide_float = guide_image.astype(jnp.float32)
    guide_pad = pad_all(guide_float)
    average, inverse = window_stats(guide_pad)
    weights = BASE_WEIGHT + pixel_mask.astype(jnp.float32) * certainty

    def operate(field_map):
        coef = coefficients(pad_all(field_map[None]), guide_pad, average, inverse)
        return apply_operator(field_map, pad_all(coef), guide_float, weights)

    mixture = seed_map
    residual = weights * seed_map - operate(seed_map)
    direction = residual
    norm_now = jnp.sum(residual * residual)
    for iteration in range(ITERS):
        image_dir = operate(direction)
        step_size = norm_now / jnp.sum(direction * image_dir)
        mixture = mixture + step_size * direction
        residual = residual - step_size * image_dir
        norm_next = jnp.sum(residual * residual)
        direction = residual + (norm_next / norm_now) * direction
        norm_now = norm_next
    return mixture
```

```python
import functools

import jax
import jax.numpy as jnp
from jax import lax
from jax.experimental import pallas as pl
from jax.experimental.pallas import tpu as pltpu
from jax.sharding import PartitionSpec as P

RIDGE = 0.05
BASE_WEIGHT = 0.1
F32 = jnp.float32
BF16 = jnp.bfloat16
MESH = pl.DeviceIdType.MESH
DIRS = ((0, 1), (0, -1), (1, 0), (-1, 0), (1, 1), (1, -1), (-1, 1), (-1, -1))
SIDE = {1: 2, -1: 1, 0: 0}
HALO = 8


def box(x):
    v = x + pltpu.roll(x, 1, 0) + pltpu.roll(x, x.shape[0] - 1, 0)
    return v + pltpu.roll(v, 1, 1) + pltpu.roll(v, x.shape[1] - 1, 1)


def window_stats(g, inside9):
    avg = [box(c) * (1.0 / 9.0) for c in g]
    second = [box(g[i] * g[j]) * (1.0 / 9.0) for i, j in ((0, 0), (0, 1), (0, 2), (1, 1), (1, 2), (2, 2))]
    rr = second[0] - avg[0] * avg[0] + RIDGE
    rg = second[1] - avg[0] * avg[1]
    rb = second[2] - avg[0] * avg[2]
    gg = second[3] - avg[1] * avg[1] + RIDGE
    gb = second[4] - avg[1] * avg[2]
    bb = second[5] - avg[2] * avg[2] + RIDGE
    c_rr = gg * bb - gb * gb
    c_rg = rb * gb - rg * bb
    c_rb = rg * gb - rb * gg
    c_gg = rr * bb - rb * rb
    c_gb = rg * rb - rr * gb
    c_bb = rr * gg - rg * rg
    det = rr * c_rr + rg * c_rg + rb * c_rb
    scale = inside9 / det
    return avg, [c * scale for c in (c_rr, c_rg, c_rb, c_gg, c_gb, c_bb)]


def smooth(p, g, avg, inv, inside9):
    pb = box(p)
    x = [box(g[i] * p) - avg[i] * pb for i in range(3)]
    s0 = inv[0] * x[0] + inv[1] * x[1] + inv[2] * x[2]
    s1 = inv[1] * x[0] + inv[3] * x[1] + inv[4] * x[2]
    s2 = inv[2] * x[0] + inv[4] * x[1] + inv[5] * x[2]
    off = pb * inside9 - (s0 * avg[0] + s1 * avg[1] + s2 * avg[2])
    return box(s0) * g[0] + box(s1) * g[1] + box(s2) * g[2] + box(off)


def kernel(sizes, f_ref, g_ref, w_ref, hw_ref, m_ref, o_ref,
           wide, ft, edge, e_in, gbuf, sw, wmat, logit, mbuf, m_in, mtile, part, parts, obuf, o_in,
           f_send, f_recv, e_send, e_recv, g_send, g_recv, s_send, s_recv,
           m_send, m_recv, p_send, p_recv, o_send, o_recv):
    n_rows, n_cols, n_sub, chans, mids, th, tw, strip = sizes
    n_c = n_cols * n_sub
    n_all = n_rows * n_c
    row = lax.axis_index("rows")
    col = lax.axis_index("cols") * n_sub + lax.axis_index("sub")
    me = row * n_c + col

    def device(r, c):
        return {"rows": r, "cols": c // n_sub, "sub": c % n_sub}

    def exists(dy, dx):
        ok = None
        for pos, step, count in ((row, dy, n_rows), (col, dx, n_c)):
            if step:
                one = (pos + step < count) if step > 0 else (pos + step >= 0)
                ok = one if ok is None else jnp.logical_and(ok, one)
        return ok

    def neighbours(pick, make):
        def start():
            for d, (dy, dx) in enumerate(DIRS):
                if pick(dy, dx):
                    @pl.when(exists(dy, dx))
                    def _(d=d, dy=dy, dx=dx):
                        make(d, dy, dx, device(row + dy, col + dx)).start()

        def finish(sent):
            for d, (dy, dx) in enumerate(DIRS):
                if pick(dy, dx):
                    ey, ex = (dy, dx) if sent else (-dy, -dx)

                    @pl.when(exists(ey, ex))
                    def _(d=d, dy=dy, dx=dx):
                        copy = make(d, dy, dx, device(row + dy, col + dx))
                        if sent:
                            copy.wait_send()
                        else:
                            copy.wait_recv()

        return start, lambda: finish(False), lambda: finish(True)

    def field_copy(buf, send, recv):
        def make(d, dy, dx, dev):
            if dy == 0:
                src, dst = pl.ds(HALO, th), pl.ds(HALO, th)
            elif dy > 0:
                src, dst = pl.ds(th, HALO), pl.ds(0, HALO)
            else:
                src, dst = pl.ds(HALO, HALO), pl.ds(HALO + th, HALO)
            return pltpu.make_async_remote_copy(
                src_ref=buf.at[0, :, src, :], dst_ref=buf.at[SIDE[dx], :, dst, :],
                send_sem=send.at[d], recv_sem=recv.at[d], device_id=dev, device_id_type=MESH)
        return make

    def row_copy(d, dy, dx, dev):
        src, dst = (th * chans, 0) if dy > 0 else (chans, (th + 1) * chans)
        return pltpu.make_async_remote_copy(
            src_ref=ft.at[pl.ds(src, chans), :], dst_ref=ft.at[pl.ds(dst, chans), :],
            send_sem=f_send.at[d], recv_sem=f_recv.at[d], device_id=dev, device_id_type=MESH)

    def edge_copy(d, dy, dx, dev):
        return pltpu.make_async_remote_copy(
            src_ref=edge, dst_ref=e_in.at[d],
            send_sem=e_send.at[d], recv_sem=e_recv.at[d], device_id=dev, device_id_type=MESH)

    def across(src, dst, send, recv):
        def make(i):
            peer = lax.rem(col + i, n_c)
            return pltpu.make_async_remote_copy(
                src_ref=src.at[peer], dst_ref=dst.at[col],
                send_sem=send.at[i], recv_sem=recv.at[i],
                device_id=device(row, peer), device_id_type=MESH)
        return make

    def share(i):
        peer = lax.rem(me + i, n_all)
        return pltpu.make_async_remote_copy(
            src_ref=part, dst_ref=parts.at[me],
            send_sem=p_send.at[i], recv_sem=p_recv.at[i],
            device_id=device(peer // n_c, peer % n_c), device_id_type=MESH)

    gbuf[...] = jnp.zeros_like(gbuf)
    sw[...] = jnp.zeros_like(sw)
    e_in[...] = jnp.zeros_like(e_in)
    zero_row = jnp.zeros((chans, tw), BF16)
    ft[pl.ds(0, chans), :] = zero_row
    ft[pl.ds((th + 1) * chans, chans), :] = zero_row

    barrier = pltpu.get_barrier_semaphore()

    @pl.loop(1, n_all)
    def _(i):
        peer = lax.rem(me + i, n_all)
        pl.semaphore_signal(barrier, inc=1, device_id=device(peer // n_c, peer % n_c), device_id_type=MESH)

    for k in range(3):
        gbuf[0, k, pl.ds(HALO, th), :] = g_ref[k].astype(F32)
    for k in range(n_c):
        mbuf[k] = m_ref[:, k * tw:(k + 1) * tw].astype(F32)
    m_in[col] = mbuf[col]

    lane = lax.broadcasted_iota(jnp.int32, (chans, tw), 1)
    rows_at_once = 256

    @pl.loop(0, chans * th // rows_at_once)
    def _(i):
        at = pl.ds(pl.multiple_of(i * rows_at_once, rows_at_once), rows_at_once)
        wide[at, :] = f_ref[at, :].astype(F32)

    def one_row(y, acc):
        cells = wide[pl.ds(y, chans, stride=th), :]
        ft[pl.ds(pl.multiple_of((y + 1) * chans, chans), chans), :] = cells.astype(BF16)
        turned = pltpu.roll(cells, 2 * y + 2, 1)
        return jnp.where((lane == 2 * y + 1) | (lane == 2 * y + 2), turned, acc)

    edge[...] = lax.fori_loop(0, th, one_row, jnp.zeros((chans, tw), F32)).astype(BF16)

    pl.semaphore_wait(barrier, n_all - 1)

    rows_go, rows_come, rows_gone = neighbours(lambda dy, dx: dx == 0, row_copy)
    edge_go, edge_come, edge_gone = neighbours(lambda dy, dx: dx != 0, edge_copy)
    guide_go, guide_come, guide_gone = neighbours(lambda dy, dx: True, field_copy(gbuf, g_send, g_recv))
    sw_go, sw_come, sw_gone = neighbours(lambda dy, dx: True, field_copy(sw, s_send, s_recv))
    mask_copy = across(mbuf, m_in, m_send, m_recv)
    out_copy = across(obuf, o_in, o_send, o_recv)

    edge_go()
    rows_go()
    guide_go()
    for i in range(1, n_c):
        mask_copy(i).start()

    for v in range(3):
        for u in range(3):
            wmat[v * mids:(v + 1) * mids, u * chans:(u + 1) * chans] = w_ref[u, v]
    eye = lax.broadcasted_iota(jnp.int32, (mids, mids), 0) == lax.broadcasted_iota(jnp.int32, (mids, mids), 1)
    head = [
        jnp.broadcast_to(
            jnp.sum(jnp.where(eye, jnp.broadcast_to(hw_ref[k:k + 1, :], (mids, mids)), 0.0), axis=1, keepdims=True),
            (mids, tw))
        for k in range(2)
    ]

    edge_come()
    odd = lane % 2 == 1

    def sides(dy):
        from_left = e_in[DIRS.index((dy, 1))].astype(F32)
        from_right = e_in[DIRS.index((dy, -1))].astype(F32)
        return jnp.where(odd, from_left, from_right)

    rim = jnp.where((lane >= 1) & (lane <= 2 * th), sides(0), 0.0)
    rim = jnp.where((lane == tw - 1) | (lane == 0), pltpu.roll(sides(1), tw - 2 * th, 1), rim)
    rim = jnp.where((lane == 2 * th + 1) | (lane == 2 * th + 2), pltpu.roll(sides(-1), 2 * th, 1), rim)
    rim3 = jnp.concatenate([pltpu.roll(rim, 2, 1), rim, pltpu.roll(rim, tw - 2, 1)], axis=0).astype(BF16)
    from_left = jnp.dot(wmat[0:mids, :], rim3, preferred_element_type=F32)
    from_right = jnp.dot(wmat[2 * mids:3 * mids, :], rim3, preferred_element_type=F32)
    rim_sum = jnp.where(odd[:mids], pltpu.roll(from_left, 2, 1), from_right)
    lane_m = lane[:mids]

    rows_come()

    @pl.loop(0, th // 2)
    def _(t):
        y0 = t * 2
        rhs = jnp.concatenate(
            [ft[pl.ds(pl.multiple_of((y0 + j) * chans, chans), 3 * chans), :] for j in range(2)], axis=1)
        prod = jnp.dot(wmat[...], rhs, preferred_element_type=F32)
        for j in range(2):
            y = y0 + j
            p = prod[:, j * tw:(j + 1) * tw]
            here = pltpu.roll(rim_sum, lax.rem(2 * tw - (2 * y + 3), tw), 1)
            conv = (p[mids:2 * mids]
                    + jnp.where(lane_m == 0, here, pltpu.roll(p[:mids], 1, 1))
                    + jnp.where(lane_m == tw - 1, here, pltpu.roll(p[2 * mids:], tw - 1, 1)))
            hidden = jnp.maximum(conv, 0.0)
            for k in range(2):
                logit[k, pl.ds(y, 1), :] = jnp.sum(hidden * head[k], axis=0, keepdims=True)

    for i in range(1, n_c):
        mask_copy(i).wait_recv()
    for k in range(n_c):
        mtile[k * strip:(k + 1) * strip, :] = m_in[k]

    seed = 1.0 / (1.0 + jnp.exp(-logit[0]))
    raw = logit[1]
    confidence = jnp.maximum(raw, 0.0) + jnp.log(1.0 + jnp.exp(-jnp.abs(raw)))
    sw[0, 0, pl.ds(HALO, th), :] = seed
    sw[0, 1, pl.ds(HALO, th), :] = BASE_WEIGHT + mtile[...] * confidence
    sw_go()

    ext_h = th + 2 * HALO
    lane_e = lax.broadcasted_iota(jnp.int32, (ext_h, tw), 1)

    def extended(buf, k):
        return jnp.concatenate([buf[0, k], jnp.where(lane_e < tw // 2, buf[1, k], buf[2, k])], axis=1)

    at_row = lax.broadcasted_iota(jnp.int32, (ext_h, 2 * tw), 0) + (row * th - HALO)
    at_col = lax.broadcasted_iota(jnp.int32, (ext_h, 2 * tw), 1)
    at_col = jnp.where(at_col >= tw + tw // 2, at_col - 2 * tw, at_col) + col * tw
    inside = (at_row >= 0) & (at_row < n_rows * th) & (at_col >= 0) & (at_col < n_c * tw)
    inside9 = jnp.where(inside, 1.0 / 9.0, 0.0)

    guide_come()
    g = [extended(gbuf, k) for k in range(3)]
    avg, inv = window_stats(g, inside9)

    sw_come()
    s = extended(sw, 0)
    w = extended(sw, 1)
    r = jnp.where(inside, smooth(s, g, avg, inv, inside9) - 9.0 * s, 0.0)
    q = jnp.where(inside, (9.0 + w) * r - smooth(r, g, avg, inv, inside9), 0.0)
    aq = (9.0 + w) * q - smooth(q, g, avg, inv, inside9)

    def core(x):
        return x[HALO:HALO + th, :tw]

    r, q, aq = core(r), core(q), core(aq)
    part[...] = jnp.zeros_like(part)
    for k, x in enumerate((r * r, r * q, q * q, q * aq)):
        part[k:k + 1, :] = jnp.sum(x, axis=0, keepdims=True)
    parts[me] = part[...]

    @pl.loop(1, n_all)
    def _(i):
        share(i).start()

    @pl.loop(1, n_all)
    def _(i):
        share(i).wait_recv()

    total = jnp.sum(jnp.sum(parts[...], axis=0), axis=1, keepdims=True)
    rr, rq, qq, qaq = (total[k:k + 1, :] for k in range(4))
    a0 = rr / rq
    rr1 = a0 * a0 * qq - rr
    b1 = 1.0 + rr1 / rr
    a1 = rr1 / (b1 * b1 * rq - 2.0 * a0 * b1 * qq + a0 * a0 * qaq)
    mixture = core(s) + (a0 + a1 * b1) * r - (a0 * a1) * q

    for k in range(n_c):
        obuf[k] = mixture[k * strip:(k + 1) * strip, :]
    o_in[col] = obuf[col]
    for i in range(1, n_c):
        out_copy(i).start()

    edge_gone()
    rows_gone()
    guide_gone()
    sw_gone()

    @pl.loop(1, n_all)
    def _(i):
        share(i).wait_send()

    for i in range(1, n_c):
        mask_copy(i).wait_send()
        out_copy(i).wait_recv()
    for k in range(n_c):
        o_ref[:, k * tw:(k + 1) * tw] = o_in[k]
    for i in range(1, n_c):
        out_copy(i).wait_send()


def on_device(mesh, features, guide_image, conv_weight, head_weight, pixel_mask):
    chans, th, tw = features.shape
    mids = conv_weight.shape[2]
    strip = pixel_mask.shape[0]
    n_rows, n_cols, n_sub = (mesh.shape[a] for a in ("rows", "cols", "sub"))
    n_c = n_cols * n_sub
    n_all = n_rows * n_c
    sizes = (n_rows, n_cols, n_sub, chans, mids, th, tw, strip)
    dma = pltpu.SemaphoreType.DMA
    vmem = pl.BlockSpec(memory_space=pltpu.VMEM)
    ext_h = th + 2 * HALO
    return pl.pallas_call(
        functools.partial(kernel, sizes),
        out_shape=jax.ShapeDtypeStruct((strip, n_c * tw), F32),
        in_specs=[vmem] * 5,
        out_specs=vmem,
        scratch_shapes=[
            pltpu.VMEM((chans * th, tw), F32),
            pltpu.VMEM(((th + 2) * chans, tw), BF16),
            pltpu.VMEM((chans, tw), BF16),
            pltpu.VMEM((8, chans, tw), BF16),
            pltpu.VMEM((3, 3, ext_h, tw), F32),
            pltpu.VMEM((3, 2, ext_h, tw), F32),
            pltpu.VMEM((3 * mids, 3 * chans), BF16),
            pltpu.VMEM((2, th, tw), F32),
            pltpu.VMEM((n_c, strip, tw), F32),
            pltpu.VMEM((n_c, strip, tw), F32),
            pltpu.VMEM((th, tw), F32),
            pltpu.VMEM((8, tw), F32),
            pltpu.VMEM((n_all, 8, tw), F32),
            pltpu.VMEM((n_c, strip, tw), F32),
            pltpu.VMEM((n_c, strip, tw), F32),
            dma((8,)), dma((8,)), dma((8,)), dma((8,)), dma((8,)), dma((8,)), dma((8,)), dma((8,)),
            dma((n_c,)), dma((n_c,)), dma((n_all,)), dma((n_all,)), dma((n_c,)), dma((n_c,)),
        ],
        compiler_params=pltpu.CompilerParams(
            collective_id=0, has_side_effects=True, vmem_limit_bytes=40 * 1024 * 1024),
    )(features.reshape(chans * th, tw), guide_image, conv_weight, head_weight, pixel_mask)


def solution(mesh):
    return jax.shard_map(
        functools.partial(on_device, mesh),
        mesh=mesh,
        in_specs=(
            P(None, ("groups", "rows"), ("cols", "sub")),
            P(None, ("groups", "rows"), ("cols", "sub")),
            P(),
            P(),
            P(("groups", "rows", "cols", "sub"), None),
        ),
        out_specs=P(("groups", "rows", "cols", "sub"), None),
        check_vma=False,
    )
```
